32 devices in a mesh: groups: 2 (over x), seg: 16 (over z, y, core).
Axes of the slice: x: 2, y: 2, z: 4, core: 2. Of those that a mesh axis runs over, the one named last changes fastest.
Arguments:
- bins: bfloat16 [1024, 128], P(('groups', 'seg')), parts along dimension 0, may hold values from -6 to 6
- conv_weight: bfloat16 [3, 128, 128], replicated, may hold values from -0.3125 to 0.3125
- conv_bias: float32 [128], replicated, may hold values from -3 to 3
- pair_left: bfloat16 [128, 48], replicated, may hold values from -0.5 to 0.5
- pair_right: bfloat16 [128, 48], replicated, may hold values from -0.5 to 0.5
- pair_weight: bfloat16 [3, 3, 48, 48], replicated, may hold values from -0.3125 to 0.3125
- pair_bias: float32 [48], replicated, may hold values from -3 to 3
- head: bfloat16 [48], replicated, may hold values from -0.875 to 0.875
- shifts: int32 [4], replicated, may hold values from -8 to 8, as said below
- flags: int32 [4], replicated, may hold values from 0 to 1, as said below
- dilations: int32 [2], replicated, may hold values from 1 to 4, as said below
Outputs:
- contacts: float32 [1024, 512], P(('groups', 'seg')), parts along dimension 0
The draws below stay inside these ranges and needn't reach their ends.
There are 2 independent parts, one for each index of `groups`. The reference program is written for one: setup_inputs(seed, part) draws one part's arguments, and reference() takes and returns one part's arrays. A program takes and returns all parts, laid end to end along the dimension named above; an argument that names none is the same for every part. Nothing has to cross between parts.
Inputs may be any that keep to these rules, and one draw needn't show every extreme that they name: `shifts`: the largest entry is 8 and the smallest -8. `flags`: exactly half of the views are reverse-complemented. `dilations`: one of the two rates equals 4 and the other is smaller.
All inputs are finite; a program needn't handle non-finite values.
Results may differ from the reference program's by a relative error of at most 0.0055.
Values may be sent and summed in bfloat16 or wider, within the bound.
A program may use at most 128 MiB of HBM per device.

```python
import jax
import jax.numpy as jnp
from jax import lax

CHANNELS = 128
PAIR_CH = 48
BAND = 512
VIEWS = 4
SHIFT = 8
DMAX = 4
LBINS = 512
HALO = 12


def draw_shifts(key, part):
    first_key, second_key = jax.random.split(jax.random.fold_in(key, 11))
    values = jax.random.randint(first_key, (VIEWS,), -SHIFT, SHIFT + 1)
    order = jax.random.permutation(second_key, VIEWS)
    values = values.at[order[0]].set(SHIFT)
    values = values.at[order[1]].set(-SHIFT)
    return values.astype(jnp.int32)


def draw_flags(key, part):
    order = jax.random.permutation(jax.random.fold_in(key, 23), VIEWS)
    return (order % 2).astype(jnp.int32)


def draw_dilations(key, part):
    first_key, second_key = jax.random.split(jax.random.fold_in(key, 37))
    others = jax.random.randint(first_key, (2,), 1, DMAX)
    which = jax.random.randint(second_key, (), 0, 2)
    return jnp.where(jnp.arange(2) == which, DMAX, others).astype(jnp.int32)


def block_levels(key, dims, cuts, least, top_value):
    def one(dim, parts):
        draws = jax.random.uniform(jax.random.fold_in(jax.random.fold_in(key, 6), dim), (parts,), jnp.float32, least / len(cuts), top_value / len(cuts))
        return jnp.repeat(jnp.exp(draws), dims[dim] // parts).reshape((-1,) + (1,) * (len(dims) - dim - 1))

    gain = one(*cuts[0])
    for cut in cuts[1:]:
        gain = gain * one(*cut)
    return gain


def gaussian(key, extent, scale, bound, cuts=(), kind=jnp.bfloat16):
    result = scale * jax.random.normal(key, extent, jnp.float32)
    if cuts:
        result = result * block_levels(key, extent, cuts, -0.22, 0.18)
    return jnp.clip(result, -bound, bound).astype(kind)


def setup_inputs(seed: int = 0, part: int = 0) -> dict:
    streams_of = jax.random.split(jax.random.key(seed), 12)
    own_keys = jax.random.split(jax.random.fold_in(streams_of[11], part), 12)
    return {
        "bins": gaussian(own_keys[0], (LBINS, CHANNELS), 1.0, 6.0, ((0, 16),)),
        "conv_weight": gaussian(streams_of[1], (3, CHANNELS, CHANNELS), (3 * CHANNELS) ** -0.5, 0.3125),
        "conv_bias": gaussian(streams_of[2], (CHANNELS,), 0.5, 3.0, (), jnp.float32),
        "pair_left": gaussian(streams_of[3], (CHANNELS, PAIR_CH), CHANNELS ** -0.5, 0.5),
        "pair_right": gaussian(streams_of[4], (CHANNELS, PAIR_CH), CHANNELS ** -0.5, 0.5),
        "pair_weight": gaussian(streams_of[5], (3, 3, PAIR_CH, PAIR_CH), (9 * PAIR_CH) ** -0.5, 0.3125),
        "pair_bias": gaussian(streams_of[6], (PAIR_CH,), 0.5, 3.0, (), jnp.float32),
        "head": gaussian(streams_of[7], (PAIR_CH,), PAIR_CH ** -0.5, 0.875),
        "shifts": draw_shifts(jax.random.fold_in(streams_of[11], 71), part),
        "flags": draw_flags(jax.random.fold_in(streams_of[11], 71), part),
        "dilations": draw_dilations(jax.random.fold_in(streams_of[11], 71), part),
    }


block_rows = 256


def view_kernels(conv_weight, flags):
    flipped = conv_weight[::-1, ::-1, :]
    chosen = (flags == 1)[:, None, None, None]
    return jnp.where(chosen, flipped[None], conv_weight[None])


def trunk(source, base, rows, shifts, dilate_seq, kernels, conv_bias, pair_left, pair_right):
    def one_view(shift, kernel):
        start = base + shift
        taps = [lax.dynamic_slice_in_dim(source, start + (tap - 1) * dilate_seq, rows, 0) for tap in range(3)]
        mixed = jnp.zeros((rows, CHANNELS), jnp.float32)
        for tap in range(3):
            mixed = mixed + jnp.dot(taps[tap].astype(jnp.float32), kernel[tap].astype(jnp.float32))
        return taps[1], mixed

    centers, mixed = jax.vmap(one_view)(shifts, kernels)
    feature = (centers.astype(jnp.float32) + jax.nn.relu(mixed + conv_bias)).astype(jnp.bfloat16)
    left = jnp.einsum("vrc,cp->vrp", feature.astype(jnp.float32), pair_left.astype(jnp.float32)).astype(jnp.bfloat16)
    right = jnp.einsum("vrc,cp->vrp", feature.astype(jnp.float32), pair_right.astype(jnp.float32)).astype(jnp.bfloat16)
    return left, right


def pair_block(left_rows, right_rows, first_row, total, dilate_pair, pair_weight, pair_bias, head):
    span = left_rows.shape[1]
    rows_out = span - 2 * DMAX
    width = right_rows.shape[1]
    global_rows = first_row + jnp.arange(span, dtype=jnp.int32)
    offsets = jnp.arange(BAND, dtype=jnp.int32)
    inside = ((global_rows >= 0) & (global_rows < total))[:, None] & ((global_rows[:, None] + offsets[None, :]) < total)
    stacked_weight = pair_weight.reshape(9 * PAIR_CH, PAIR_CH)

    def view_step(view, running):
        left = left_rows[view]
        right_cols = right_rows[view].T
        skewed = jnp.tile(right_cols, (1, span + 1))[:, : span * (width + 1)]
        skewed = skewed.reshape(PAIR_CH, span, width + 1)[:, :, :BAND]
        pairs = jax.nn.relu(left.T.astype(jnp.float32)[:, :, None] + skewed.astype(jnp.float32))
        pairs = jnp.where(inside[None], pairs, 0.0).astype(jnp.bfloat16)
        padded = jnp.pad(pairs, ((0, 0), (0, 0), (DMAX, DMAX)))
        pieces = []
        for row_tap in range(3):
            for col_tap in range(3):
                row_start = (DMAX + (row_tap - 1) * dilate_pair).astype(jnp.int32)
                col_start = (DMAX + (col_tap - 1) * dilate_pair).astype(jnp.int32)
                pieces.append(lax.dynamic_slice(padded, (jnp.int32(0), row_start, col_start), (PAIR_CH, rows_out, BAND)))
        stacked = jnp.concatenate(pieces, 0)
        summed = jnp.einsum("kid,ke->eid", stacked.astype(jnp.float32), stacked_weight.astype(jnp.float32))
        hidden = jax.nn.relu(summed + pair_bias[:, None, None])
        return running + jnp.einsum("eid,e->id", hidden, head.astype(jnp.float32))

    running = lax.fori_loop(0, VIEWS, view_step, jnp.zeros((rows_out, BAND), jnp.float32))
    return running / VIEWS


def reference(bins, conv_weight, conv_bias, pair_left, pair_right, pair_weight, pair_bias, head, shifts, flags, dilations):
    total = bins.shape[0]
    kernels = view_kernels(conv_weight, flags)
    source = jnp.pad(bins, ((HALO, HALO), (0, 0)))
    left, right = trunk(source, HALO, total, shifts, dilations[0], kernels, conv_bias, pair_left, pair_right)
    left_pad = jnp.pad(left, ((0, 0), (DMAX, DMAX), (0, 0)))
    right_pad = jnp.pad(right, ((0, 0), (DMAX, DMAX + BAND), (0, 0)))

    def one_block(number):
        start = number * block_rows
        left_rows = lax.dynamic_slice_in_dim(left_pad, start, block_rows + 2 * DMAX, 1)
        right_rows = lax.dynamic_slice_in_dim(right_pad, start, block_rows + 2 * DMAX + BAND, 1)
        return pair_block(left_rows, right_rows, start - DMAX, total, dilations[1], pair_weight, pair_bias, head)

    blocks = lax.map(one_block, jnp.arange(total // block_rows, dtype=jnp.int32))
    return blocks.reshape(total, BAND)
```

```python
import functools

import jax
import jax.numpy as jnp
from jax import lax
from jax.experimental import pallas as pl
from jax.experimental.pallas import tpu as pltpu
from jax.sharding import PartitionSpec as P

BAND = 512
DMAX = 4
OUT_ROWS = 3
IN_ROWS = OUT_ROWS + 2
WIDE = 256
LEAD = 16
TILE = 16
FAR = -1e30
F32 = jnp.float32
BF16 = jnp.bfloat16


def gather_kernel(segments, blocks, rows, x_ref, out_ref, send_sem, recv_sem, own_sem):
    me = lax.axis_index("seg")
    barrier = pltpu.get_barrier_semaphore()
    reach = min(blocks - 2, segments - 1)
    count = jnp.int32(0)
    for step in range(1, reach + 1):
        for other in (me - step, me + step):
            there = (other >= 0) & (other < segments)

            @pl.when(there)
            def _():
                pl.semaphore_signal(
                    barrier,
                    inc=1,
                    device_id={"seg": other},
                    device_id_type=pl.DeviceIdType.MESH,
                )

            count = count + there.astype(jnp.int32)
    own = pltpu.make_async_copy(x_ref, out_ref.at[pl.ds(rows, rows)], own_sem)
    own.start()
    for slot in range(blocks):
        source = me + slot - 1

        @pl.when((source < 0) | (source >= segments))
        def _():
            out_ref[pl.ds(slot * rows, rows), :] = jnp.zeros((rows, out_ref.shape[1]), BF16)

    pl.semaphore_wait(barrier, count)

    def copy(slot):
        return pltpu.make_async_remote_copy(
            src_ref=x_ref,
            dst_ref=out_ref.at[pl.ds(slot * rows, rows)],
            send_sem=send_sem.at[slot],
            recv_sem=recv_sem.at[slot],
            device_id={"seg": me - slot + 1},
            device_id_type=pl.DeviceIdType.MESH,
        )

    for slot in reversed(range(blocks)):
        target = me - slot + 1
        if slot != 1 and abs(slot - 1) <= reach:

            @pl.when((target >= 0) & (target < segments))
            def _():
                copy(slot).start()

    own.wait()
    for slot in range(blocks):
        target = me - slot + 1
        source = me + slot - 1
        if slot != 1 and abs(slot - 1) <= reach:

            @pl.when((source >= 0) & (source < segments))
            def _():
                copy(slot).wait_recv()

            @pl.when((target >= 0) & (target < segments))
            def _():
                copy(slot).wait_send()


def slot_of(index, size):
    total = jnp.zeros(index.shape, jnp.int32)
    for k in range(1, IN_ROWS):
        total = total + (index >= k * size).astype(jnp.int32)
    return total


def dot(a, b, **kw):
    return jnp.dot(a, b, preferred_element_type=F32, **kw)


def pair_kernel(
    rows,
    segments,
    shifts,
    flags,
    dilations,
    win_ref,
    cw_ref,
    cb_ref,
    pleft_ref,
    pright_ref,
    pw_ref,
    pb_ref,
    head_ref,
    out_ref,
    xf,
    kern,
    wall,
    rt,
    r5,
    r5b,
    l5,
    cols,
):
    channels = win_ref.shape[1]
    pc = pleft_ref.shape[1]
    views = shifts.shape[0]
    total = rows * segments
    base = lax.axis_index("seg") * rows
    near = rows + BAND
    frows = near + 2 * LEAD
    q = dilations[0]
    r = dilations[1]

    xf[...] = win_ref[...].astype(F32)
    ci = lax.broadcasted_iota(jnp.int32, (channels, channels), 0)
    cj = lax.broadcasted_iota(jnp.int32, (channels, channels), 1)
    mirror = jnp.where(ci + cj == channels - 1, 1.0, 0.0).astype(BF16)
    for t in range(3):
        at = slice(t * channels, (t + 1) * channels)
        kern[0, at, :] = cw_ref[t]
        kern[1, at, :] = dot(mirror, cw_ref[2 - t]).astype(BF16)

    lane = lax.broadcasted_iota(jnp.int32, (pc, WIDE), 1)
    chan = lax.broadcasted_iota(jnp.int32, (pc, WIDE), 0)
    spots = [jnp.where(lane - chan == k * pc, 1.0, 0.0) for k in range(IN_ROWS)]
    tiler_f = sum(spots[1:], spots[0])
    tiler = tiler_f.astype(BF16)
    wide_left = dot(pleft_ref[...], tiler).astype(BF16)
    wide_right = dot(pright_ref[...], tiler).astype(BF16)
    placed = [dot(pw_ref[...], spots[o].astype(BF16)) for o in range(OUT_ROWS)]
    for b in range(3):
        for k in range(IN_ROWS):
            block = jnp.zeros((pc, WIDE), F32)
            for o in range(OUT_ROWS):
                if 0 <= k - o <= 2:
                    first = ((k - o) * 3 + b) * pc
                    block = block + placed[o][first : first + pc]
            wall[b * WIDE + k * pc : b * WIDE + (k + 1) * pc, :] = block.astype(BF16)
        wall[b * WIDE + IN_ROWS * pc : (b + 1) * WIDE, :] = jnp.zeros(
            (WIDE - IN_ROWS * pc, WIDE), BF16
        )
    bias8 = jnp.broadcast_to(pb_ref[...], (8, pc))
    bias = dot(bias8, tiler_f, precision=lax.Precision.HIGHEST)[0:1, :]
    wi = lax.broadcasted_iota(jnp.int32, (WIDE, pc), 0)
    wc = lax.broadcasted_iota(jnp.int32, (WIDE, pc), 1)
    hit = wi == wc
    for o in range(1, OUT_ROWS):
        hit = hit | (wi - wc == o * pc)
    untile = jnp.where(hit, 1.0, 0.0).astype(BF16)
    head_b = jnp.broadcast_to(head_ref[...].astype(F32), (128, pc)).astype(BF16)
    head_rows = lax.dot_general(
        untile, head_b, (((1,), (1,)), ((), ())), preferred_element_type=F32
    )
    target = lax.broadcasted_iota(jnp.int32, (WIDE, 128), 1) - r * slot_of(
        lax.broadcasted_iota(jnp.int32, (WIDE, 128), 0), pc
    )

    half = lax.broadcasted_iota(jnp.int32, (1, 128), 1)

    def skew(rows_out, first):
        def at(k, side):
            return rt[side, pl.ds(first + (k - 1) * r, rows_out), :]

        low = jnp.where(half < pc, at(0, 0), jnp.where(half < 2 * pc, at(1, 0), at(2, 0)))
        up = 3 * pc - 128
        high = jnp.where(half < up, at(2, 1), jnp.where(half < up + pc, at(3, 1), at(4, 1)))
        return low, high

    grow = lax.broadcasted_iota(jnp.int32, (frows, 1), 0) + (base - LEAD)
    inside = (grow >= 0) & (grow < total)
    lrows = rows + 2 * LEAD

    def one_view(v, _):
        start = rows - LEAD + shifts[v]
        flag = flags[v]
        taps = [xf[pl.ds(start + (t - 1) * q, frows), :] for t in range(3)]
        stacked = jnp.concatenate([t.astype(BF16) for t in taps], axis=1)
        mixed = dot(stacked, kern[flag])
        feature = (taps[1] + jnp.maximum(mixed + cb_ref[...], 0.0)).astype(BF16)
        lw = dot(feature[:lrows], wide_left).astype(BF16).astype(F32)
        for side in range(2):
            part = lw[:, side * 128 : side * 128 + 128]
            rt[side, pl.ds(0, lrows), :] = jnp.where(inside[:lrows], part, FAR)
        low, high = skew(rows, LEAD)
        l5[v, 0] = low
        l5[v, 1] = high
        rw = dot(feature, wide_right).astype(BF16).astype(F32)
        for side in range(2):
            part = rw[:, side * 128 : side * 128 + 128]
            rt[side, pl.ds(0, frows), :] = jnp.where(inside, part, FAR)
        low, high = skew(near + 16, 8)
        r5[0] = low
        r5[1] = high
        for b in range(3):
            for side in range(2):
                moved = r5[side, pl.ds(8 + (b - 1) * r, near), :]
                r5b[v, b, :, side * 128 : side * 128 + 128] = moved.astype(BF16)
        return 0

    lax.fori_loop(0, views, one_view, 0)

    cols[...] = jnp.zeros_like(cols)
    span = BAND + TILE
    edge = 2 * TILE
    edge_row = lax.broadcasted_iota(jnp.int32, (edge, WIDE), 0)
    shift_row = lax.broadcasted_iota(jnp.int32, (rows, 128), 0)

    def group(g, moves):
        i0 = lax.rem(g, r) + OUT_ROWS * r * lax.div(g, r)
        nb = pl.multiple_of(lax.div(i0, TILE) * TILE, TILE)
        off = i0 - nb
        head_mask = jnp.where(edge_row - off < r, FAR, 0.0).astype(BF16)
        tail_mask = jnp.where(
            edge_row + (span - edge) - off >= BAND - r, FAR, 0.0
        ).astype(BF16)
        hidden = None
        for v in range(views):
            row = jnp.concatenate([l5[v, side, pl.ds(i0, 1), :] for side in range(2)], 1)
            row = jnp.broadcast_to(row, (TILE, WIDE)).astype(BF16)[None]
            parts = []
            for b in range(3):
                value = r5b[v, b, pl.ds(nb, span), :]
                if b == 0:
                    value = jnp.concatenate([value[:edge] + head_mask, value[edge:]], 0)
                if b == 2:
                    value = jnp.concatenate([value[:-edge], value[-edge:] + tail_mask], 0)
                value = jnp.maximum(value.reshape(span // TILE, TILE, WIDE) + row, 0)
                parts.append(value.reshape(span, WIDE))
            summed = dot(jnp.concatenate(parts, 1), wall[...])
            term = jnp.maximum(summed + bias, 0.0)
            hidden = term if hidden is None else hidden + term
        spread = jnp.where(target == i0, head_rows, 0.0).astype(BF16)
        cols[pl.ds(nb, span), :] += dot(hidden.astype(BF16), spread)
        delta = shift_row - i0
        mine = (delta == 0) | (delta == r) | (delta == 2 * r)
        return jnp.where(mine, i0, moves)

    per_class = lax.div(lax.div(rows + r - 1, r) + OUT_ROWS - 1, OUT_ROWS)
    moves = lax.fori_loop(0, r * per_class, group, jnp.zeros((rows, 128), jnp.int32))

    lanes = cols.shape[0]
    flat = cols[...].T[:rows]
    moves = jnp.concatenate([moves] * (lanes // 128), axis=1)
    bit = 1
    while bit < rows:
        flat = jnp.where((moves & bit) != 0, pltpu.roll(flat, lanes - bit, 1), flat)
        bit *= 2
    out_ref[...] = flat[:, :BAND] * (1.0 / views)


def per_device(
    bins,
    conv_weight,
    conv_bias,
    pair_left,
    pair_right,
    pair_weight,
    pair_bias,
    head,
    shifts,
    flags,
    dilations,
):
    rows, channels = bins.shape
    views = shifts.shape[0]
    pc = pair_left.shape[1]
    segments = lax.axis_size("seg")
    near = rows + BAND
    frows = near + 2 * LEAD
    blocks = 1 + -(-(near + LEAD + 3 * DMAX) // rows)
    vmem = pl.BlockSpec(memory_space=pltpu.VMEM)
    smem = pl.BlockSpec(memory_space=pltpu.SMEM)
    window = pl.pallas_call(
        functools.partial(gather_kernel, segments, blocks, rows),
        out_shape=jax.ShapeDtypeStruct((blocks * rows, channels), BF16),
        in_specs=[vmem],
        out_specs=vmem,
        scratch_shapes=[
            pltpu.SemaphoreType.DMA((blocks,)),
            pltpu.SemaphoreType.DMA((blocks,)),
            pltpu.SemaphoreType.DMA,
        ],
        compiler_params=pltpu.CompilerParams(collective_id=0, has_side_effects=True),
    )(bins)
    lanes = -(-near // 128) * 128
    return pl.pallas_call(
        functools.partial(pair_kernel, rows, segments),
        out_shape=jax.ShapeDtypeStruct((rows, BAND), F32),
        in_specs=[smem] * 3 + [vmem] * 8,
        out_specs=vmem,
        scratch_shapes=[
            pltpu.VMEM((blocks * rows, channels), F32),
            pltpu.VMEM((2, 3 * channels, channels), BF16),
            pltpu.VMEM((3 * WIDE, WIDE), BF16),
            pltpu.VMEM((2, frows + 16, 128), F32),
            pltpu.VMEM((2, near + 16, 128), F32),
            pltpu.VMEM((views, 3, near, WIDE), BF16),
            pltpu.VMEM((views, 2, rows, 128), F32),
            pltpu.VMEM((lanes, 128), F32),
        ],
        compiler_params=pltpu.CompilerParams(vmem_limit_bytes=60 * 1024 * 1024),
    )(
        shifts,
        flags,
        dilations,
        window,
        conv_weight,
        conv_bias.reshape(1, channels),
        pair_left,
        pair_right,
        pair_weight.reshape(9 * pc, pc),
        pair_bias.reshape(1, pc),
        head.reshape(1, pc),
    )


def solution(mesh):
    placed = (P(("groups", "seg"), None), P(), P(), P(), P(), P(), P(), P(), P(), P(), P())
    return jax.shard_map(
        per_device,
        mesh=mesh,
        in_specs=placed,
        out_specs=P(("groups", "seg"), None),
        check_vma=False,
    )
```

```python
import functools

import jax
import jax.numpy as jnp
from jax import lax
from jax.experimental import pallas as pl
from jax.experimental.pallas import tpu as pltpu
from jax.sharding import PartitionSpec as P

BAND = 512
DMAX = 4
OUT_ROWS = 3
IN_ROWS = OUT_ROWS + 2
WIDE = 256
LEAD = 16
TILE = 16
FAR = -1e30
F32 = jnp.float32
BF16 = jnp.bfloat16


def gather_kernel(segments, blocks, rows, x_ref, out_ref, send_sem, recv_sem, own_sem):
    me = lax.axis_index("seg")
    barrier = pltpu.get_barrier_semaphore()
    reach = min(blocks - 2, segments - 1)
    count = jnp.int32(0)
    for step in range(1, reach + 1):
        for other in (me - step, me + step):
            there = (other >= 0) & (other < segments)

            @pl.when(there)
            def _():
                pl.semaphore_signal(
                    barrier,
                    inc=1,
                    device_id={"seg": other},
                    device_id_type=pl.DeviceIdType.MESH,
                )

            count = count + there.astype(jnp.int32)
    own = pltpu.make_async_copy(x_ref, out_ref.at[pl.ds(rows, rows)], own_sem)
    own.start()
    for slot in range(blocks):
        source = me + slot - 1

        @pl.when((source < 0) | (source >= segments))
        def _():
            out_ref[pl.ds(slot * rows, rows), :] = jnp.zeros((rows, out_ref.shape[1]), BF16)

    pl.semaphore_wait(barrier, count)

    def copy(slot):
        return pltpu.make_async_remote_copy(
            src_ref=x_ref,
            dst_ref=out_ref.at[pl.ds(slot * rows, rows)],
            send_sem=send_sem.at[slot],
            recv_sem=recv_sem.at[slot],
            device_id={"seg": me - slot + 1},
            device_id_type=pl.DeviceIdType.MESH,
        )

    for slot in reversed(range(blocks)):
        target = me - slot + 1
        if slot != 1 and abs(slot - 1) <= reach:

            @pl.when((target >= 0) & (target < segments))
            def _():
                copy(slot).start()

    own.wait()
    for slot in range(blocks):
        target = me - slot + 1
        source = me + slot - 1
        if slot != 1 and abs(slot - 1) <= reach:

            @pl.when((source >= 0) & (source < segments))
            def _():
                copy(slot).wait_recv()

            @pl.when((target >= 0) & (target < segments))
            def _():
                copy(slot).wait_send()


def slot_of(index, size):
    total = jnp.zeros(index.shape, jnp.int32)
    for k in range(1, IN_ROWS):
        total = total + (index >= k * size).astype(jnp.int32)
    return total


def dot(a, b, **kw):
    return jnp.dot(a, b, preferred_element_type=F32, **kw)


def dot_t(a, b):
    return lax.dot_general(a, b, (((0,), (0,)), ((), ())), preferred_element_type=F32)


def pair_kernel(
    rows,
    segments,
    shifts,
    flags,
    dilations,
    win_ref,
    cw_ref,
    cb_ref,
    pleft_ref,
    pright_ref,
    pw_ref,
    pb_ref,
    head_ref,
    out_ref,
    xf,
    kern,
    wall,
    rt,
    r5,
    r5b,
    l5,
    cols,
):
    channels = win_ref.shape[1]
    pc = pleft_ref.shape[0]
    views = shifts.shape[0]
    total = rows * segments
    base = lax.axis_index("seg") * rows
    near = rows + BAND
    frows = near + 2 * LEAD
    q = dilations[0]
    r = dilations[1]

    xf[...] = win_ref[...].astype(F32)
    ci = lax.broadcasted_iota(jnp.int32, (channels, channels), 0)
    cj = lax.broadcasted_iota(jnp.int32, (channels, channels), 1)
    mirror = jnp.where(ci + cj == channels - 1, 1.0, 0.0).astype(BF16)
    for t in range(3):
        at = slice(t * channels, (t + 1) * channels)
        kern[0, at, :] = cw_ref[t]
        kern[1, at, :] = dot(mirror, cw_ref[2 - t]).astype(BF16)

    lane = lax.broadcasted_iota(jnp.int32, (pc, WIDE), 1)
    chan = lax.broadcasted_iota(jnp.int32, (pc, WIDE), 0)
    spots = [jnp.where(lane - chan == k * pc, 1.0, 0.0) for k in range(IN_ROWS)]
    tiler_f = sum(spots[1:], spots[0])
    tiler = tiler_f.astype(BF16)
    wide_left = dot_t(pleft_ref[...], tiler).astype(BF16)
    wide_right = dot_t(pright_ref[...], tiler).astype(BF16)
    placed = [dot(pw_ref[...], spots[o].astype(BF16)) for o in range(OUT_ROWS)]
    for b in range(3):
        for k in range(IN_ROWS):
            block = jnp.zeros((pc, WIDE), F32)
            for o in range(OUT_ROWS):
                if 0 <= k - o <= 2:
                    first = ((k - o) * 3 + b) * pc
                    block = block + placed[o][first : first + pc]
            wall[b * WIDE + k * pc : b * WIDE + (k + 1) * pc, :] = block.astype(BF16)
        wall[b * WIDE + IN_ROWS * pc : (b + 1) * WIDE, :] = jnp.zeros(
            (WIDE - IN_ROWS * pc, WIDE), BF16
        )
    bias8 = jnp.broadcast_to(pb_ref[...], (8, pc))
    bias = dot(bias8, tiler_f, precision=lax.Precision.HIGHEST)[0:1, :]
    wi = lax.broadcasted_iota(jnp.int32, (WIDE, pc), 0)
    wc = lax.broadcasted_iota(jnp.int32, (WIDE, pc), 1)
    hit = wi == wc
    for o in range(1, OUT_ROWS):
        hit = hit | (wi - wc == o * pc)
    untile = jnp.where(hit, 1.0, 0.0).astype(BF16)
    head_b = jnp.broadcast_to(head_ref[...].astype(F32), (128, pc)).astype(BF16)
    head_rows = lax.dot_general(
        untile, head_b, (((1,), (1,)), ((), ())), preferred_element_type=F32
    )
    target = lax.broadcasted_iota(jnp.int32, (WIDE, 128), 1) - r * slot_of(
        lax.broadcasted_iota(jnp.int32, (WIDE, 128), 0), pc
    )

    half = lax.broadcasted_iota(jnp.int32, (1, 128), 1)

    def skew(rows_out, first):
        def at(k, side):
            return rt[side, pl.ds(first + (k - 1) * r, rows_out), :]

        low = jnp.where(half < pc, at(0, 0), jnp.where(half < 2 * pc, at(1, 0), at(2, 0)))
        up = 3 * pc - 128
        high = jnp.where(half < up, at(2, 1), jnp.where(half < up + pc, at(3, 1), at(4, 1)))
        return low, high

    grow = lax.broadcasted_iota(jnp.int32, (frows, 1), 0) + (base - LEAD)
    inside = (grow >= 0) & (grow < total)
    lrows = rows + 2 * LEAD

    def one_view(v, _):
        start = rows - LEAD + shifts[v]
        flag = flags[v]
        taps = [xf[pl.ds(start + (t - 1) * q, frows), :] for t in range(3)]
        stacked = jnp.concatenate([t.astype(BF16) for t in taps], axis=1)
        mixed = dot(stacked, kern[flag])
        feature = (taps[1] + jnp.maximum(mixed + cb_ref[...], 0.0)).astype(BF16)
        lw = dot(feature[:lrows], wide_left).astype(BF16).astype(F32)
        for side in range(2):
            part = lw[:, side * 128 : side * 128 + 128]
            rt[side, pl.ds(0, lrows), :] = jnp.where(inside[:lrows], part, FAR)
        low, high = skew(rows, LEAD)
        l5[v, 0] = low
        l5[v, 1] = high
        rw = dot(feature, wide_right).astype(BF16).astype(F32)
        for side in range(2):
            part = rw[:, side * 128 : side * 128 + 128]
            rt[side, pl.ds(0, frows), :] = jnp.where(inside, part, FAR)
        low, high = skew(near + 16, 8)
        r5[0] = low
        r5[1] = high
        for b in range(3):
            for side in range(2):
                moved = r5[side, pl.ds(8 + (b - 1) * r, near), :]
                r5b[v, b, :, side * 128 : side * 128 + 128] = moved.astype(BF16)
        return 0

    lax.fori_loop(0, views, one_view, 0)

    cols[...] = jnp.zeros_like(cols)
    span = BAND + TILE
    edge = 2 * TILE
    edge_row = lax.broadcasted_iota(jnp.int32, (edge, WIDE), 0)
    shift_row = lax.broadcasted_iota(jnp.int32, (rows, 128), 0)

    def group(g, moves):
        i0 = lax.rem(g, r) + OUT_ROWS * r * lax.div(g, r)
        nb = pl.multiple_of(lax.div(i0, TILE) * TILE, TILE)
        off = i0 - nb
        head_mask = jnp.where(edge_row - off < r, FAR, 0.0).astype(BF16)
        tail_mask = jnp.where(
            edge_row + (span - edge) - off >= BAND - r, FAR, 0.0
        ).astype(BF16)
        hidden = None
        for v in range(views):
            row = jnp.concatenate([l5[v, side, pl.ds(i0, 1), :] for side in range(2)], 1)
            row = jnp.broadcast_to(row, (TILE, WIDE)).astype(BF16)[None]
            parts = []
            for b in range(3):
                value = r5b[v, b, pl.ds(nb, span), :]
                if b == 0:
                    value = jnp.concatenate([value[:edge] + head_mask, value[edge:]], 0)
                if b == 2:
                    value = jnp.concatenate([value[:-edge], value[-edge:] + tail_mask], 0)
                value = jnp.maximum(value.reshape(span // TILE, TILE, WIDE) + row, 0)
                parts.append(value.reshape(span, WIDE))
            summed = dot(jnp.concatenate(parts, 1), wall[...])
            term = jnp.maximum(summed + bias, 0.0)
            hidden = term if hidden is None else hidden + term
        spread = jnp.where(target == i0, head_rows, 0.0).astype(BF16)
        cols[pl.ds(nb, span), :] += dot(hidden.astype(BF16), spread)
        delta = shift_row - i0
        mine = (delta == 0) | (delta == r) | (delta == 2 * r)
        return jnp.where(mine, i0, moves)

    per_class = lax.div(lax.div(rows + r - 1, r) + OUT_ROWS - 1, OUT_ROWS)
    moves = lax.fori_loop(0, r * per_class, group, jnp.zeros((rows, 128), jnp.int32))

    lanes = cols.shape[0]
    flat = cols[...].T[:rows]
    moves = jnp.concatenate([moves] * (lanes // 128), axis=1)
    bit = 1
    while bit < rows:
        flat = jnp.where((moves & bit) != 0, pltpu.roll(flat, lanes - bit, 1), flat)
        bit *= 2
    out_ref[...] = flat[:, :BAND] * (1.0 / views)


def per_device(
    bins,
    conv_weight,
    conv_bias,
    pair_left,
    pair_right,
    pair_weight,
    pair_bias,
    head,
    shifts,
    flags,
    dilations,
):
    rows, channels = bins.shape
    views = shifts.shape[0]
    pc = pair_left.shape[1]
    segments = lax.axis_size("seg")
    near = rows + BAND
    frows = near + 2 * LEAD
    blocks = 1 + -(-(near + LEAD + 3 * DMAX) // rows)
    vmem = pl.BlockSpec(memory_space=pltpu.VMEM)
    smem = pl.BlockSpec(memory_space=pltpu.SMEM)
    window = pl.pallas_call(
        functools.partial(gather_kernel, segments, blocks, rows),
        out_shape=jax.ShapeDtypeStruct((blocks * rows, channels), BF16),
        in_specs=[vmem],
        out_specs=vmem,
        scratch_shapes=[
            pltpu.SemaphoreType.DMA((blocks,)),
            pltpu.SemaphoreType.DMA((blocks,)),
            pltpu.SemaphoreType.DMA,
        ],
        compiler_params=pltpu.CompilerParams(collective_id=0, has_side_effects=True),
    )(bins)
    lanes = -(-near // 128) * 128
    return pl.pallas_call(
        functools.partial(pair_kernel, rows, segments),
        out_shape=jax.ShapeDtypeStruct((rows, BAND), F32),
        in_specs=[smem] * 3 + [vmem] * 8,
        out_specs=vmem,
        scratch_shapes=[
            pltpu.VMEM((blocks * rows, channels), F32),
            pltpu.VMEM((2, 3 * channels, channels), BF16),
            pltpu.VMEM((3 * WIDE, WIDE), BF16),
            pltpu.VMEM((2, frows + 16, 128), F32),
            pltpu.VMEM((2, near + 16, 128), F32),
            pltpu.VMEM((views, 3, near, WIDE), BF16),
            pltpu.VMEM((views, 2, rows, 128), F32),
            pltpu.VMEM((lanes, 128), F32),
        ],
        compiler_params=pltpu.CompilerParams(vmem_limit_bytes=60 * 1024 * 1024),
    )(
        shifts,
        flags,
        dilations,
        window,
        conv_weight,
        conv_bias.reshape(1, channels),
        pair_left.T,
        pair_right.T,
        pair_weight.reshape(9 * pc, pc),
        pair_bias.reshape(1, pc),
        head.reshape(1, pc),
    )


def solution(mesh):
    placed = (P(("groups", "seg"), None), P(), P(), P(), P(), P(), P(), P(), P(), P(), P())
    return jax.shard_map(
        per_device,
        mesh=mesh,
        in_specs=placed,
        out_specs=P(("groups", "seg"), None),
        check_vma=False,
    )
```

```python
import functools

import jax
import jax.numpy as jnp
from jax import lax
from jax.experimental import pallas as pl
from jax.experimental.pallas import tpu as pltpu
from jax.sharding import PartitionSpec as P

BAND = 512
DMAX = 4
OUT_ROWS = 3
IN_ROWS = OUT_ROWS + 2
WIDE = 256
LEAD = 16
TILE = 16
FAR = -1e30
F32 = jnp.float32
BF16 = jnp.bfloat16


def gather_kernel(segments, blocks, rows, x_ref, out_ref, send_sem, recv_sem, own_sem):
    me = lax.axis_index("seg")
    barrier = pltpu.get_barrier_semaphore()
    reach = min(blocks - 2, segments - 1)
    count = jnp.int32(0)
    for step in range(1, reach + 1):
        for other in (me - step, me + step):
            there = (other >= 0) & (other < segments)

            @pl.when(there)
            def _():
                pl.semaphore_signal(
                    barrier,
                    inc=1,
                    device_id={"seg": other},
                    device_id_type=pl.DeviceIdType.MESH,
                )

            count = count + there.astype(jnp.int32)
    own = pltpu.make_async_copy(x_ref, out_ref.at[pl.ds(rows, rows)], own_sem)
    own.start()
    for slot in range(blocks):
        source = me + slot - 1

        @pl.when((source < 0) | (source >= segments))
        def _():
            out_ref[pl.ds(slot * rows, rows), :] = jnp.zeros((rows, out_ref.shape[1]), BF16)

    pl.semaphore_wait(barrier, count)

    def copy(slot):
        return pltpu.make_async_remote_copy(
            src_ref=x_ref,
            dst_ref=out_ref.at[pl.ds(slot * rows, rows)],
            send_sem=send_sem.at[slot],
            recv_sem=recv_sem.at[slot],
            device_id={"seg": me - slot + 1},
            device_id_type=pl.DeviceIdType.MESH,
        )

    for slot in reversed(range(blocks)):
        target = me - slot + 1
        if slot != 1 and abs(slot - 1) <= reach:

            @pl.when((target >= 0) & (target < segments))
            def _():
                copy(slot).start()

    own.wait()
    for slot in range(blocks):
        target = me - slot + 1
        source = me + slot - 1
        if slot != 1 and abs(slot - 1) <= reach:

            @pl.when((source >= 0) & (source < segments))
            def _():
                copy(slot).wait_recv()

            @pl.when((target >= 0) & (target < segments))
            def _():
                copy(slot).wait_send()


def slot_of(index, size):
    total = jnp.zeros(index.shape, jnp.int32)
    for k in range(1, IN_ROWS):
        total = total + (index >= k * size).astype(jnp.int32)
    return total


def dot(a, b, **kw):
    return jnp.dot(a, b, preferred_element_type=F32, **kw)


def dot_t(a, b):
    return lax.dot_general(a, b, (((0,), (0,)), ((), ())), preferred_element_type=F32)


def pair_kernel(
    rows,
    segments,
    shifts,
    flags,
    dilations,
    win_ref,
    cw_ref,
    cb_ref,
    pleft_ref,
    pright_ref,
    pw_ref,
    pb_ref,
    head_ref,
    out_ref,
    xf,
    kern,
    wall,
    l5,
    cols,
    *per_view,
):
    channels = win_ref.shape[1]
    pc = pleft_ref.shape[0]
    views = shifts.shape[0]
    total = rows * segments
    base = lax.axis_index("seg") * rows
    near = rows + BAND
    frows = near + 2 * LEAD
    q = dilations[0]
    r = dilations[1]

    xf[...] = win_ref[...].astype(F32)
    ci = lax.broadcasted_iota(jnp.int32, (channels, channels), 0)
    cj = lax.broadcasted_iota(jnp.int32, (channels, channels), 1)
    mirror = jnp.where(ci + cj == channels - 1, 1.0, 0.0).astype(BF16)
    for t in range(3):
        at = slice(t * channels, (t + 1) * channels)
        kern[0, at, :] = cw_ref[t]
        kern[1, at, :] = dot(mirror, cw_ref[2 - t]).astype(BF16)

    lane = lax.broadcasted_iota(jnp.int32, (pc, WIDE), 1)
    chan = lax.broadcasted_iota(jnp.int32, (pc, WIDE), 0)
    spots = [jnp.where(lane - chan == k * pc, 1.0, 0.0) for k in range(IN_ROWS)]
    tiler_f = sum(spots[1:], spots[0])
    tiler = tiler_f.astype(BF16)
    wide_left = dot_t(pleft_ref[...], tiler).astype(BF16)
    wide_right = dot_t(pright_ref[...], tiler).astype(BF16)
    placed = [dot(pw_ref[...], spots[o].astype(BF16)) for o in range(OUT_ROWS)]
    for b in range(3):
        for k in range(IN_ROWS):
            block = jnp.zeros((pc, WIDE), F32)
            for o in range(OUT_ROWS):
                if 0 <= k - o <= 2:
                    first = ((k - o) * 3 + b) * pc
                    block = block + placed[o][first : first + pc]
            wall[b * WIDE + k * pc : b * WIDE + (k + 1) * pc, :] = block.astype(BF16)
        wall[b * WIDE + IN_ROWS * pc : (b + 1) * WIDE, :] = jnp.zeros(
            (WIDE - IN_ROWS * pc, WIDE), BF16
        )
    bias8 = jnp.broadcast_to(pb_ref[...], (8, pc))
    bias = dot(bias8, tiler_f, precision=lax.Precision.HIGHEST)[0:1, :]
    wi = lax.broadcasted_iota(jnp.int32, (WIDE, pc), 0)
    wc = lax.broadcasted_iota(jnp.int32, (WIDE, pc), 1)
    hit = wi == wc
    for o in range(1, OUT_ROWS):
        hit = hit | (wi - wc == o * pc)
    untile = jnp.where(hit, 1.0, 0.0).astype(BF16)
    head_b = jnp.broadcast_to(head_ref[...].astype(F32), (128, pc)).astype(BF16)
    head_rows = lax.dot_general(
        untile, head_b, (((1,), (1,)), ((), ())), preferred_element_type=F32
    )
    target = lax.broadcasted_iota(jnp.int32, (WIDE, 128), 1) - r * slot_of(
        lax.broadcasted_iota(jnp.int32, (WIDE, 128), 0), pc
    )

    half = lax.broadcasted_iota(jnp.int32, (1, 128), 1)

    def skew(rt, rows_out, first):
        def at(k, side):
            return rt[side, pl.ds(first + (k - 1) * r, rows_out), :]

        low = jnp.where(half < pc, at(0, 0), jnp.where(half < 2 * pc, at(1, 0), at(2, 0)))
        up = 3 * pc - 128
        high = jnp.where(half < up, at(2, 1), jnp.where(half < up + pc, at(3, 1), at(4, 1)))
        return low, high

    grow = lax.broadcasted_iota(jnp.int32, (frows, 1), 0) + (base - LEAD)
    inside = (grow >= 0) & (grow < total)
    lrows = rows + 2 * LEAD

    def one_view(v):
        lt, rt, r5, r5b = per_view[4 * v : 4 * v + 4]
        start = rows - LEAD + shifts[v]
        flag = flags[v]
        taps = [xf[pl.ds(start + (t - 1) * q, frows), :] for t in range(3)]
        stacked = jnp.concatenate([t.astype(BF16) for t in taps], axis=1)
        mixed = dot(stacked, kern[flag])
        feature = (taps[1] + jnp.maximum(mixed + cb_ref[...], 0.0)).astype(BF16)
        lw = dot(feature[:lrows], wide_left).astype(BF16).astype(F32)
        for side in range(2):
            part = lw[:, side * 128 : side * 128 + 128]
            lt[side] = jnp.where(inside[:lrows], part, FAR)
        low, high = skew(lt, rows, LEAD)
        l5[v, 0] = low
        l5[v, 1] = high
        rw = dot(feature, wide_right).astype(BF16).astype(F32)
        for side in range(2):
            part = rw[:, side * 128 : side * 128 + 128]
            rt[side, pl.ds(0, frows), :] = jnp.where(inside, part, FAR)
        low, high = skew(rt, near + 16, 8)
        r5[0] = low
        r5[1] = high
        for b in range(3):
            for side in range(2):
                moved = r5[side, pl.ds(8 + (b - 1) * r, near), :]
                r5b[b, :, side * 128 : side * 128 + 128] = moved.astype(BF16)

    for v in range(views):
        one_view(v)

    cols[...] = jnp.zeros_like(cols)
    span = BAND + TILE
    edge = 2 * TILE
    edge_row = lax.broadcasted_iota(jnp.int32, (edge, WIDE), 0)
    shift_row = lax.broadcasted_iota(jnp.int32, (rows, 128), 0)

    def group(g, moves):
        i0 = lax.rem(g, r) + OUT_ROWS * r * lax.div(g, r)
        nb = pl.multiple_of(lax.div(i0, TILE) * TILE, TILE)
        off = i0 - nb
        head_mask = jnp.where(edge_row - off < r, FAR, 0.0).astype(BF16)
        tail_mask = jnp.where(
            edge_row + (span - edge) - off >= BAND - r, FAR, 0.0
        ).astype(BF16)
        hidden = None
        for v in range(views):
            row = jnp.concatenate([l5[v, side, pl.ds(i0, 1), :] for side in range(2)], 1)
            row = jnp.broadcast_to(row, (TILE, WIDE)).astype(BF16)[None]
            parts = []
            for b in range(3):
                value = per_view[4 * v + 3][b, pl.ds(nb, span), :]
                if b == 0:
                    value = jnp.concatenate([value[:edge] + head_mask, value[edge:]], 0)
                if b == 2:
                    value = jnp.concatenate([value[:-edge], value[-edge:] + tail_mask], 0)
                value = jnp.maximum(value.reshape(span // TILE, TILE, WIDE) + row, 0)
                parts.append(value.reshape(span, WIDE))
            summed = dot(jnp.concatenate(parts, 1), wall[...])
            term = jnp.maximum(summed + bias, 0.0)
            hidden = term if hidden is None else hidden + term
        spread = jnp.where(target == i0, head_rows, 0.0).astype(BF16)
        cols[pl.ds(nb, span), :] += dot(hidden.astype(BF16), spread)
        delta = shift_row - i0
        mine = (delta == 0) | (delta == r) | (delta == 2 * r)
        return jnp.where(mine, i0, moves)

    per_class = lax.div(lax.div(rows + r - 1, r) + OUT_ROWS - 1, OUT_ROWS)
    moves = lax.fori_loop(0, r * per_class, group, jnp.zeros((rows, 128), jnp.int32))

    lanes = cols.shape[0]
    flat = cols[...].T[:rows]
    moves = jnp.concatenate([moves] * (lanes // 128), axis=1)
    bit = 1
    while bit < rows:
        flat = jnp.where((moves & bit) != 0, pltpu.roll(flat, lanes - bit, 1), flat)
        bit *= 2
    out_ref[...] = flat[:, :BAND] * (1.0 / views)


def per_device(
    bins,
    conv_weight,
    conv_bias,
    pair_left,
    pair_right,
    pair_weight,
    pair_bias,
    head,
    shifts,
    flags,
    dilations,
):
    rows, channels = bins.shape
    views = shifts.shape[0]
    pc = pair_left.shape[1]
    segments = lax.axis_size("seg")
    near = rows + BAND
    frows = near + 2 * LEAD
    blocks = 1 + -(-(near + LEAD + 3 * DMAX) // rows)
    vmem = pl.BlockSpec(memory_space=pltpu.VMEM)
    smem = pl.BlockSpec(memory_space=pltpu.SMEM)
    window = pl.pallas_call(
        functools.partial(gather_kernel, segments, blocks, rows),
        out_shape=jax.ShapeDtypeStruct((blocks * rows, channels), BF16),
        in_specs=[vmem],
        out_specs=vmem,
        scratch_shapes=[
            pltpu.SemaphoreType.DMA((blocks,)),
            pltpu.SemaphoreType.DMA((blocks,)),
            pltpu.SemaphoreType.DMA,
        ],
        compiler_params=pltpu.CompilerParams(collective_id=0, has_side_effects=True),
    )(bins)
    lanes = -(-near // 128) * 128
    return pl.pallas_call(
        functools.partial(pair_kernel, rows, segments),
        out_shape=jax.ShapeDtypeStruct((rows, BAND), F32),
        in_specs=[smem] * 3 + [vmem] * 8,
        out_specs=vmem,
        scratch_shapes=[
            pltpu.VMEM((blocks * rows, channels), F32),
            pltpu.VMEM((2, 3 * channels, channels), BF16),
            pltpu.VMEM((3 * WIDE, WIDE), BF16),
            pltpu.VMEM((views, 2, rows, 128), F32),
            pltpu.VMEM((lanes, 128), F32),
        ]
        + [
            pltpu.VMEM((2, rows + 2 * LEAD, 128), F32),
            pltpu.VMEM((2, frows + 16, 128), F32),
            pltpu.VMEM((2, near + 16, 128), F32),
            pltpu.VMEM((3, near, WIDE), BF16),
        ]
        * views,
        compiler_params=pltpu.CompilerParams(vmem_limit_bytes=60 * 1024 * 1024),
    )(
        shifts,
        flags,
        dilations,
        window,
        conv_weight,
        conv_bias.reshape(1, channels),
        pair_left.T,
        pair_right.T,
        pair_weight.reshape(9 * pc, pc),
        pair_bias.reshape(1, pc),
        head.reshape(1, pc),
    )


def solution(mesh):
    placed = (P(("groups", "seg"), None), P(), P(), P(), P(), P(), P(), P(), P(), P(), P())
    return jax.shard_map(
        per_device,
        mesh=mesh,
        in_specs=placed,
        out_specs=P(("groups", "seg"), None),
        check_vma=False,
    )
```

```python
import functools

import jax
import jax.numpy as jnp
from jax import lax
from jax.experimental import pallas as pl
from jax.experimental.pallas import tpu as pltpu
from jax.sharding import PartitionSpec as P

BAND = 512
DMAX = 4
OUT_ROWS = 3
IN_ROWS = OUT_ROWS + 2
WIDE = 256
LEAD = 16
TILE = 16
FAR = -1e30
F32 = jnp.float32
BF16 = jnp.bfloat16


def gather_kernel(segments, blocks, rows, x_ref, out_ref, send_sem, recv_sem, own_sem):
    me = lax.axis_index("seg")
    barrier = pltpu.get_barrier_semaphore()
    reach = min(blocks - 2, segments - 1)
    count = jnp.int32(0)
    for step in range(1, reach + 1):
        for other in (me - step, me + step):
            there = (other >= 0) & (other < segments)

            @pl.when(there)
            def _():
                pl.semaphore_signal(
                    barrier,
                    inc=1,
                    device_id={"seg": other},
                    device_id_type=pl.DeviceIdType.MESH,
                )

            count = count + there.astype(jnp.int32)
    own = pltpu.make_async_copy(x_ref, out_ref.at[pl.ds(rows, rows)], own_sem)
    own.start()
    for slot in range(blocks):
        source = me + slot - 1

        @pl.when((source < 0) | (source >= segments))
        def _():
            out_ref[pl.ds(slot * rows, rows), :] = jnp.zeros((rows, out_ref.shape[1]), BF16)

    pl.semaphore_wait(barrier, count)

    def copy(slot):
        return pltpu.make_async_remote_copy(
            src_ref=x_ref,
            dst_ref=out_ref.at[pl.ds(slot * rows, rows)],
            send_sem=send_sem.at[slot],
            recv_sem=recv_sem.at[slot],
            device_id={"seg": me - slot + 1},
            device_id_type=pl.DeviceIdType.MESH,
        )

    for slot in reversed(range(blocks)):
        target = me - slot + 1
        if slot != 1 and abs(slot - 1) <= reach:

            @pl.when((target >= 0) & (target < segments))
            def _():
                copy(slot).start()

    own.wait()
    for slot in range(blocks):
        target = me - slot + 1
        source = me + slot - 1
        if slot != 1 and abs(slot - 1) <= reach:

            @pl.when((source >= 0) & (source < segments))
            def _():
                copy(slot).wait_recv()

            @pl.when((target >= 0) & (target < segments))
            def _():
                copy(slot).wait_send()


def slot_of(index, size):
    total = jnp.zeros(index.shape, jnp.int32)
    for k in range(1, IN_ROWS):
        total = total + (index >= k * size).astype(jnp.int32)
    return total


def dot(a, b, **kw):
    return jnp.dot(a, b, preferred_element_type=F32, **kw)


def dot_t(a, b):
    return lax.dot_general(a, b, (((0,), (0,)), ((), ())), preferred_element_type=F32)


def pair_kernel(
    rows,
    segments,
    shifts,
    flags,
    dilations,
    win_ref,
    cw_ref,
    cb_ref,
    pleft_ref,
    pright_ref,
    pw_ref,
    pb_ref,
    head_ref,
    out_ref,
    xf,
    kern,
    wall,
    l5,
    cols,
    *per_view,
):
    channels = win_ref.shape[1]
    pc = pleft_ref.shape[0]
    views = shifts.shape[0]
    total = rows * segments
    base = lax.axis_index("seg") * rows
    near = rows + BAND
    frows = near + 2 * LEAD
    q = dilations[0]
    r = dilations[1]

    xf[...] = win_ref[...].astype(F32)
    ci = lax.broadcasted_iota(jnp.int32, (channels, channels), 0)
    cj = lax.broadcasted_iota(jnp.int32, (channels, channels), 1)
    mirror = jnp.where(ci + cj == channels - 1, 1.0, 0.0).astype(BF16)
    for t in range(3):
        at = slice(t * channels, (t + 1) * channels)
        kern[0, at, :] = cw_ref[t]
        kern[1, at, :] = dot(mirror, cw_ref[2 - t]).astype(BF16)

    lane = lax.broadcasted_iota(jnp.int32, (pc, WIDE), 1)
    chan = lax.broadcasted_iota(jnp.int32, (pc, WIDE), 0)
    spots = [jnp.where(lane - chan == k * pc, 1.0, 0.0) for k in range(IN_ROWS)]
    tiler_f = sum(spots[1:], spots[0])
    tiler = tiler_f.astype(BF16)
    wide_left = dot_t(pleft_ref[...], tiler).astype(BF16)
    wide_right = dot_t(pright_ref[...], tiler).astype(BF16)
    placed = [dot(pw_ref[...], spots[o].astype(BF16)) for o in range(OUT_ROWS)]
    for b in range(3):
        for k in range(IN_ROWS):
            block = jnp.zeros((pc, WIDE), F32)
            for o in range(OUT_ROWS):
                if 0 <= k - o <= 2:
                    first = ((k - o) * 3 + b) * pc
                    block = block + placed[o][first : first + pc]
            wall[b * WIDE + k * pc : b * WIDE + (k + 1) * pc, :] = block.astype(BF16)
        wall[b * WIDE + IN_ROWS * pc : (b + 1) * WIDE, :] = jnp.zeros(
            (WIDE - IN_ROWS * pc, WIDE), BF16
        )
    bias8 = jnp.broadcast_to(pb_ref[...], (8, pc))
    bias = dot(bias8, tiler_f, precision=lax.Precision.HIGHEST)[0:1, :]
    wi = lax.broadcasted_iota(jnp.int32, (WIDE, pc), 0)
    wc = lax.broadcasted_iota(jnp.int32, (WIDE, pc), 1)
    hit = wi == wc
    for o in range(1, OUT_ROWS):
        hit = hit | (wi - wc == o * pc)
    untile = jnp.where(hit, 1.0, 0.0).astype(BF16)
    head_b = jnp.broadcast_to(head_ref[...].astype(F32), (128, pc)).astype(BF16)
    head_rows = lax.dot_general(
        untile, head_b, (((1,), (1,)), ((), ())), preferred_element_type=F32
    )
    target = lax.broadcasted_iota(jnp.int32, (WIDE, 128), 1) - r * slot_of(
        lax.broadcasted_iota(jnp.int32, (WIDE, 128), 0), pc
    )

    half = lax.broadcasted_iota(jnp.int32, (1, 128), 1)

    def skew(rt, rows_out, first):
        def at(k, side):
            return rt[side, pl.ds(first + (k - 1) * r, rows_out), :]

        low = jnp.where(half < pc, at(0, 0), jnp.where(half < 2 * pc, at(1, 0), at(2, 0)))
        up = 3 * pc - 128
        high = jnp.where(half < up, at(2, 1), jnp.where(half < up + pc, at(3, 1), at(4, 1)))
        return low, high

    grow = lax.broadcasted_iota(jnp.int32, (frows, 1), 0) + (base - LEAD)
    inside = (grow >= 0) & (grow < total)
    lrows = rows + 2 * LEAD

    def one_view(v):
        lt, rt, r5, r5b = per_view[4 * v : 4 * v + 4]
        start = rows - LEAD + shifts[v]
        flag = flags[v]
        taps = [xf[pl.ds(start + (t - 1) * q, frows), :] for t in range(3)]
        stacked = jnp.concatenate([t.astype(BF16) for t in taps], axis=1)
        mixed = dot(stacked, kern[flag])
        feature = (taps[1] + jnp.maximum(mixed + cb_ref[...], 0.0)).astype(BF16)
        lw = dot(feature[:lrows], wide_left).astype(BF16).astype(F32)
        for side in range(2):
            part = lw[:, side * 128 : side * 128 + 128]
            lt[side] = jnp.where(inside[:lrows], part, FAR)
        low, high = skew(lt, rows, LEAD)
        l5[v, 0] = low
        l5[v, 1] = high
        rw = dot(feature, wide_right).astype(BF16).astype(F32)
        for side in range(2):
            part = rw[:, side * 128 : side * 128 + 128]
            rt[side, pl.ds(0, frows), :] = jnp.where(inside, part, FAR)
        low, high = skew(rt, near + 16, 8)
        r5[0] = low
        r5[1] = high
        for b in range(3):
            for side in range(2):
                if b == 1:
                    moved = (low, high)[side][8 : 8 + near]
                else:
                    moved = r5[side, pl.ds(8 + (b - 1) * r, near), :]
                r5b[b, :, side * 128 : side * 128 + 128] = moved.astype(BF16)

    for v in range(views):
        one_view(v)

    cols[...] = jnp.zeros_like(cols)
    span = BAND + TILE
    edge = 2 * TILE
    edge_row = lax.broadcasted_iota(jnp.int32, (edge, WIDE), 0)
    shift_row = lax.broadcasted_iota(jnp.int32, (rows, 128), 0)

    def group(g, moves):
        i0 = lax.rem(g, r) + OUT_ROWS * r * lax.div(g, r)
        nb = pl.multiple_of(lax.div(i0, TILE) * TILE, TILE)
        off = i0 - nb
        head_mask = jnp.where(edge_row - off < r, FAR, 0.0).astype(BF16)
        tail_mask = jnp.where(
            edge_row + (span - edge) - off >= BAND - r, FAR, 0.0
        ).astype(BF16)
        hidden = None
        for v in range(views):
            row = jnp.concatenate([l5[v, side, pl.ds(i0, 1), :] for side in range(2)], 1)
            row = jnp.broadcast_to(row, (TILE, WIDE)).astype(BF16)[None]
            parts = []
            for b in range(3):
                value = per_view[4 * v + 3][b, pl.ds(nb, span), :]
                if b == 0:
                    value = jnp.concatenate([value[:edge] + head_mask, value[edge:]], 0)
                if b == 2:
                    value = jnp.concatenate([value[:-edge], value[-edge:] + tail_mask], 0)
                value = jnp.maximum(value.reshape(span // TILE, TILE, WIDE) + row, 0)
                parts.append(value.reshape(span, WIDE))
            summed = dot(jnp.concatenate(parts, 1), wall[...])
            term = jnp.maximum(summed + bias, 0.0)
            hidden = term if hidden is None else hidden + term
        spread = jnp.where(target == i0, head_rows, 0.0).astype(BF16)
        cols[pl.ds(nb, span), :] += dot(hidden.astype(BF16), spread)
        delta = shift_row - i0
        mine = (delta == 0) | (delta == r) | (delta == 2 * r)
        return jnp.where(mine, i0, moves)

    per_class = lax.div(lax.div(rows + r - 1, r) + OUT_ROWS - 1, OUT_ROWS)
    moves = lax.fori_loop(0, r * per_class, group, jnp.zeros((rows, 128), jnp.int32))

    lanes = cols.shape[0]
    flat = cols[...].T[:rows]
    moves = jnp.concatenate([moves] * (lanes // 128), axis=1)
    bit = 1
    while bit < rows:
        flat = jnp.where((moves & bit) != 0, pltpu.roll(flat, lanes - bit, 1), flat)
        bit *= 2
    out_ref[...] = flat[:, :BAND] * (1.0 / views)


def per_device(
    bins,
    conv_weight,
    conv_bias,
    pair_left,
    pair_right,
    pair_weight,
    pair_bias,
    head,
    shifts,
    flags,
    dilations,
):
    rows, channels = bins.shape
    views = shifts.shape[0]
    pc = pair_left.shape[1]
    segments = lax.axis_size("seg")
    near = rows + BAND
    frows = near + 2 * LEAD
    blocks = 1 + -(-(near + LEAD + 3 * DMAX) // rows)
    vmem = pl.BlockSpec(memory_space=pltpu.VMEM)
    smem = pl.BlockSpec(memory_space=pltpu.SMEM)
    window = pl.pallas_call(
        functools.partial(gather_kernel, segments, blocks, rows),
        out_shape=jax.ShapeDtypeStruct((blocks * rows, channels), BF16),
        in_specs=[vmem],
        out_specs=vmem,
        scratch_shapes=[
            pltpu.SemaphoreType.DMA((blocks,)),
            pltpu.SemaphoreType.DMA((blocks,)),
            pltpu.SemaphoreType.DMA,
        ],
        compiler_params=pltpu.CompilerParams(collective_id=0, has_side_effects=True),
    )(bins)
    lanes = -(-near // 128) * 128
    return pl.pallas_call(
        functools.partial(pair_kernel, rows, segments),
        out_shape=jax.ShapeDtypeStruct((rows, BAND), F32),
        in_specs=[smem] * 3 + [vmem] * 8,
        out_specs=vmem,
        scratch_shapes=[
            pltpu.VMEM((blocks * rows, channels), F32),
            pltpu.VMEM((2, 3 * channels, channels), BF16),
            pltpu.VMEM((3 * WIDE, WIDE), BF16),
            pltpu.VMEM((views, 2, rows, 128), F32),
            pltpu.VMEM((lanes, 128), F32),
        ]
        + [
            pltpu.VMEM((2, rows + 2 * LEAD, 128), F32),
            pltpu.VMEM((2, frows + 16, 128), F32),
            pltpu.VMEM((2, near + 16, 128), F32),
            pltpu.VMEM((3, near, WIDE), BF16),
        ]
        * views,
        compiler_params=pltpu.CompilerParams(vmem_limit_bytes=60 * 1024 * 1024),
    )(
        shifts,
        flags,
        dilations,
        window,
        conv_weight,
        conv_bias.reshape(1, channels),
        pair_left.T,
        pair_right.T,
        pair_weight.reshape(9 * pc, pc),
        pair_bias.reshape(1, pc),
        head.reshape(1, pc),
    )


def solution(mesh):
    placed = (P(("groups", "seg"), None), P(), P(), P(), P(), P(), P(), P(), P(), P(), P())
    return jax.shard_map(
        per_device,
        mesh=mesh,
        in_specs=placed,
        out_specs=P(("groups", "seg"), None),
        check_vma=False,
    )
```
